32 devices in a mesh: dom: 16 (over z, y, core), ch: 2 (over x).
Axes of the slice: x: 2, y: 2, z: 4, core: 2. Of those that a mesh axis runs over, the one named last changes fastest.
Arguments:
- node_irreps: bfloat16 [49, 128, 256], P(None, 'ch', 'dom'), may hold values from -6 to 6
- out_grad: bfloat16 [49, 128, 256], P(None, 'ch', 'dom'), may hold values from -6 to 6
- edge_source: int32 [8, 256], P(None, 'dom'), may hold values from 0 to 31
- edge_rotation: int32 [8, 256], P(None, 'dom'), may hold values from 0 to 255
- edge_count: int32 [256], P('dom'), may hold values from 1 to 8
- ghost_slot: int32 [256], P('dom'), may hold values from 0 to 15, as said below
- wigner: float32 [455, 4096], P(None, 'dom'), may hold values from -1 to 1, as said below
- so2_m0: bfloat16 [7, 128, 7, 128], P(None, 'ch'), may hold values from -0.1875 to 0.1875
- so2_m1: bfloat16 [2, 6, 128, 6, 128], P(None, None, 'ch'), may hold values from -0.15625 to 0.15625
- so2_m2: bfloat16 [2, 5, 128, 5, 128], P(None, None, 'ch'), may hold values from -0.15625 to 0.15625
- attn_vector: float32 [128], P('ch'), may hold values from -60 to 60
Outputs:
- updated: bfloat16 [49, 128, 256], P(None, 'ch', 'dom')
- irreps_grad: float32 [49, 128, 256], P(None, 'ch', 'dom')
The draws below stay inside these ranges and needn't reach their ends.
Inputs may be any that keep to these rules, and one draw needn't show every extreme that they name: `edge_source`: slots below 16 are the domain's own atoms in order; slot 16 + g is the domain's ghost g. `edge_rotation`: picks one of the 256 columns of wigner that belong to the atom's domain. Slots j < edge_count[a] are live, the others padding. `ghost_slot`: of a domain's 16 entries, the first 8 name atoms of the previous domain (cyclically) among its last 16 slots, the others atoms of the next domain among its first 16 slots. `wigner`: each column holds for l = 0..6 an orthogonal (2l+1) x (2l+1) block, row-major, blocks in order of l.
All inputs are finite; a program needn't handle non-finite values.
Results may differ from the reference program's by a relative error of at most 0.012.
The reference program's roundings to bfloat16 on the way (of `rot`) count: a program that leaves them out, or rounds other values in their place, can miss the bound.
Values may be sent and summed in bfloat16 or wider, within the bound.
A program may use at most 128 MiB of HBM per device.

```python
import jax
import jax.numpy as jnp
from jax import lax

C = 128
HEADS = 8
LMAX = 6
MMAX = 2
OWN = 16
NB = 8
GH = 16
RIM = 16
ROT_DOM = 256
K = 49
HEAD_CH = 16
ATOMS = 256
ROTATIONS = 4096
N_DOM = 16
N_CH = 2


def draw_ghost_slot(key, part):
    half = GH // 2
    low = jax.random.randint(jax.random.fold_in(key, 101), (N_DOM, half), OWN - RIM, OWN, dtype=jnp.int32)
    high = jax.random.randint(jax.random.fold_in(key, 102), (N_DOM, GH - half), 0, RIM, dtype=jnp.int32)
    return jnp.concatenate([low, high], 1).reshape(N_DOM * GH)


def draw_wigner(key, part):
    pieces = []
    for level in range(LMAX + 1):
        width = 2 * level + 1
        raw = jax.random.normal(jax.random.fold_in(key, 211 + level), (ROTATIONS, width, width), jnp.float32) * 0.6
        skewed = raw - jnp.swapaxes(raw, 1, 2)
        eye = jnp.broadcast_to(jnp.eye(width, dtype=jnp.float32), (ROTATIONS, width, width))
        ortho = jnp.linalg.solve(eye + skewed, eye - skewed)
        pieces.append(ortho.reshape(ROTATIONS, width * width).T)
    return jnp.concatenate(pieces, 0).astype(jnp.float32)


def draw_attn_vector(key, part):
    base = jnp.clip(jax.random.normal(jax.random.fold_in(key, 301), (C,), jnp.float32), -4.0, 4.0) * HEAD_CH ** (-0.5)
    return base.astype(jnp.float32)


def touch_ends(result, key, low, high):
    spot = [jax.random.randint(jax.random.fold_in(key, axis), (), 0, length) for axis, length in enumerate(result.shape)]
    longest = result.shape.index(max(result.shape))
    beside = spot[:longest] + [(spot[longest] + 1) % result.shape[longest]] + spot[longest + 1:]
    return result.at[tuple(spot)].set(low).at[tuple(beside)].set(high)


def level_of(key, dims, cuts, least, top_value):
    gain = 1.0
    for dim, blocks in cuts:
        heights = jax.random.uniform(jax.random.fold_in(jax.random.fold_in(key, 6), dim), (blocks,), jnp.float32, least / len(cuts), top_value / len(cuts))
        gain = gain * jnp.repeat(jnp.exp(heights), dims[dim] // blocks).reshape((-1,) + (1,) * (len(dims) - 1 - dim))
    return gain


def noise(key, shape, scale, most, split=(), kind=jnp.bfloat16):
    drawn = jax.random.normal(key, shape, jnp.float32) * scale
    if len(split) > 0:
        drawn = level_of(key, shape, split, -0.22, 0.18) * drawn
    return jnp.clip(drawn, min=-most, max=most).astype(kind)


def setup_inputs(seed: int = 0) -> dict:
    key_of = jax.random.split(jax.random.key(seed), 12)
    return {
        "node_irreps": noise(key_of[0], (K, C, ATOMS), 1.0, 6.0, ((1, 2), (2, 16))),
        "out_grad": noise(key_of[1], (K, C, ATOMS), 1.0, 6.0, ((1, 2), (2, 16))),
        "edge_source": touch_ends(jax.random.randint(key_of[2], (NB, ATOMS), 0, OWN + GH), jax.random.fold_in(key_of[2], 1), 0, (OWN + GH) - 1).astype(jnp.int32),
        "edge_rotation": touch_ends(jax.random.randint(key_of[3], (NB, ATOMS), 0, ROT_DOM), jax.random.fold_in(key_of[3], 1), 0, ROT_DOM - 1).astype(jnp.int32),
        "edge_count": touch_ends(jax.random.randint(key_of[4], (ATOMS,), 1, NB + 1), jax.random.fold_in(key_of[4], 1), 1, NB).astype(jnp.int32),
        "ghost_slot": draw_ghost_slot(jax.random.fold_in(key_of[11], 71), 0),
        "wigner": draw_wigner(jax.random.fold_in(key_of[11], 71), 0),
        "so2_m0": noise(key_of[7], (LMAX + 1, C, LMAX + 1, C), ((LMAX + 1) * C) ** -0.5, 0.1875, ((1, 2),)),
        "so2_m1": noise(key_of[8], (2, LMAX, C, LMAX, C), (2 * LMAX * C) ** -0.5, 0.15625, ((2, 2),)),
        "so2_m2": noise(key_of[9], (2, LMAX - 1, C, LMAX - 1, C), (2 * (LMAX - 1) * C) ** -0.5, 0.15625, ((2, 2),)),
        "attn_vector": draw_attn_vector(jax.random.fold_in(key_of[11], 71), 0),
    }


def plan_tables(degree_top, order_top):
    blocks = []
    offset = 0
    lmajor = []
    for level in range(degree_top + 1):
        width = 2 * level + 1
        reach = min(level, order_top)
        kept = [level + order for order in range(-reach, reach + 1)]
        blocks.append((level, width, offset, kept))
        for order in range(-reach, reach + 1):
            lmajor.append((level, order))
        offset += width * width
    grouped = [(level, 0) for level in range(degree_top + 1)]
    for order in range(1, order_top + 1):
        grouped += [(level, order) for level in range(order, degree_top + 1)]
        grouped += [(level, -order) for level in range(order, degree_top + 1)]
    to_group = [lmajor.index(entry) for entry in grouped]
    to_major = [grouped.index(entry) for entry in lmajor]
    return (blocks, to_group, to_major)

def rotate_in(feats, wig_edges, blocks, to_group):
    parts = []
    for level, width, offset, kept in blocks:
        for row in kept:
            acc = wig_edges[offset + row * width][None, :] * feats[level * level]
            for col in range(1, width):
                acc = acc + wig_edges[offset + row * width + col][None, :] * feats[level * level + col]
            parts.append(acc)
    return jnp.stack([parts[i] for i in to_group])

def rotate_out(values, wig_edges, blocks, to_major):
    rows = [values[i] for i in to_major]
    out = []
    pos = 0
    for level, width, offset, kept in blocks:
        mine = rows[pos:pos + len(kept)]
        pos += len(kept)
        for col in range(width):
            acc = wig_edges[offset + kept[0] * width + col][None, :] * mine[0]
            for j in range(1, len(kept)):
                acc = acc + wig_edges[offset + kept[j] * width + col][None, :] * mine[j]
            out.append(acc)
    return jnp.stack(out)

def so2_mix(rot, w_zero, w_one, w_two, degree_top):
    chans = rot.shape[1]
    edges = rot.shape[2]
    group = w_zero.shape[1]
    first = degree_top + 1
    outs = [jnp.dot(w_zero.reshape(first * group, first * chans).astype(jnp.float32), rot[:first].reshape(first * chans, edges).astype(jnp.float32), preferred_element_type=jnp.float32).reshape(first, group, edges)]
    pos = first
    for order, weights in ((1, w_one), (2, w_two)):
        count = degree_top + 1 - order
        plus = rot[pos:pos + count].reshape(count * chans, edges)
        minus = rot[pos + count:pos + 2 * count].reshape(count * chans, edges)
        real = weights[0].reshape(count * group, count * chans)
        imag = weights[1].reshape(count * group, count * chans)
        y_plus = jnp.dot(real.astype(jnp.float32), plus.astype(jnp.float32), preferred_element_type=jnp.float32) - jnp.dot(imag.astype(jnp.float32), minus.astype(jnp.float32), preferred_element_type=jnp.float32)
        y_minus = jnp.dot(real.astype(jnp.float32), minus.astype(jnp.float32), preferred_element_type=jnp.float32) + jnp.dot(imag.astype(jnp.float32), plus.astype(jnp.float32), preferred_element_type=jnp.float32)
        outs += [y_plus.reshape(count, group, edges), y_minus.reshape(count, group, edges)]
        pos += 2 * count
    return jnp.concatenate(outs, 0)

def attend_tail(rot32, wig_edges, counts, w_zero, w_one, w_two, attn, heads_here, blocks, to_major, degree_top):
    rot = rot32.astype(jnp.bfloat16)
    mixed = so2_mix(rot, w_zero, w_one, w_two, degree_top)
    scalar = mixed[0]
    values = mixed * jax.nn.sigmoid(scalar)[None]
    group, edges = scalar.shape
    atoms_here = counts.shape[0]
    slots = edges // atoms_here
    score = (jax.nn.silu(scalar) * attn[:, None]).reshape(heads_here, group // heads_here, edges).sum(1)
    score = score.reshape(heads_here, slots, atoms_here)
    live = (lax.broadcasted_iota(jnp.int32, (slots, atoms_here), 0) < counts[None, :])[None]
    top = lax.optimization_barrier(jnp.max(jnp.where(live, score, -1e+30), axis=1, keepdims=True))
    weight = jnp.exp(jnp.where(live, score - top, -1e+30))
    weight = weight / lax.optimization_barrier(jnp.sum(weight, axis=1, keepdims=True))
    spread = jnp.broadcast_to(weight.reshape(heads_here, 1, edges), (heads_here, group // heads_here, edges)).reshape(group, edges)
    back = rotate_out(values * spread[None], wig_edges, blocks, to_major)
    return back.reshape(back.shape[0], group, slots, atoms_here).sum(2)

def reference(node_irreps, out_grad, edge_source, edge_rotation, edge_count, ghost_slot, wigner, so2_m0, so2_m1, so2_m2, attn_vector):
    blocks, to_group, to_major = plan_tables(LMAX, MMAX)
    group = C // N_CH
    heads_here = HEADS // N_CH
    slots = ghost_slot.reshape(N_DOM, GH)
    half = GH // 2

    def one_domain(x32, d):
        lower = jnp.mod(d - 1, N_DOM).astype(jnp.int32)
        upper = jnp.mod(d + 1, N_DOM).astype(jnp.int32)
        own = lax.dynamic_slice_in_dim(x32, (d * OWN).astype(jnp.int32), OWN, 2)
        below = jnp.take(lax.dynamic_slice_in_dim(x32, (lower * OWN).astype(jnp.int32), OWN, 2), slots[d, :half], axis=2)
        above = jnp.take(lax.dynamic_slice_in_dim(x32, (upper * OWN).astype(jnp.int32), OWN, 2), slots[d, half:], axis=2)
        table = jnp.concatenate([own, below, above], 2)
        source = lax.dynamic_slice_in_dim(edge_source, (d * OWN).astype(jnp.int32), OWN, 1).reshape(-1)
        turn = lax.dynamic_slice_in_dim(edge_rotation, (d * OWN).astype(jnp.int32), OWN, 1).reshape(-1)
        counts = lax.dynamic_slice_in_dim(edge_count, (d * OWN).astype(jnp.int32), OWN, 0)
        table_rot = lax.dynamic_slice_in_dim(wigner, (d * ROT_DOM).astype(jnp.int32), ROT_DOM, 1)
        wig_edges = jnp.take(table_rot, turn, axis=1)
        feats = jnp.take(table, source, axis=2)
        outs = []
        for index in range(N_CH):
            lo = index * group
            rot32 = rotate_in(feats, wig_edges, blocks, to_group)
            outs.append(attend_tail(rot32, wig_edges, counts, so2_m0[:, lo:lo + group], so2_m1[:, :, lo:lo + group], so2_m2[:, :, lo:lo + group], attn_vector[lo:lo + group], heads_here, blocks, to_major, LMAX))
        return jnp.concatenate(outs, 1)

    def forward(x32):
        stacked = lax.map(lambda d: jax.checkpoint(one_domain)(x32, d), jnp.arange(N_DOM, dtype=jnp.int32))
        return jnp.transpose(stacked, (1, 2, 0, 3)).reshape(K, C, ATOMS)
    x32 = node_irreps.astype(jnp.float32)
    agg, pullback = jax.vjp(forward, x32)
    updated = (x32 + agg).astype(jnp.bfloat16)
    grad32 = out_grad.astype(jnp.float32)
    irreps_grad = grad32 + pullback(grad32)[0]
    return (updated, irreps_grad)
```

```python
import functools

import jax
import jax.numpy as jnp
from jax import lax
from jax.experimental import pallas as pl
from jax.experimental.pallas import tpu as pltpu
from jax.sharding import PartitionSpec as P

HEADS = 8
LMAX = 6
MMAX = 2
CHUNK = 16
MESH = pl.DeviceIdType.MESH
VMEM = pltpu.VMEM
BF = jnp.bfloat16
F32 = jnp.float32


def degree_blocks():
    out = []
    offset = 0
    for level in range(LMAX + 1):
        width = 2 * level + 1
        reach = min(level, MMAX)
        out.append((level, width, offset, list(range(-reach, reach + 1))))
        offset += width * width
    return out


BLOCKS = degree_blocks()


def dot(a, b, dims):
    return lax.dot_general(a, b, (dims, ((), ())), preferred_element_type=F32)


def nn(a, b):
    return dot(a, b, ((1,), (0,)))


def nt(a, b):
    return dot(a, b, ((1,), (1,)))


def tn(a, b):
    return dot(a, b, ((0,), (0,)))


def iota(shape, dim):
    return lax.broadcasted_iota(jnp.int32, shape, dim)


def eye(n, dtype):
    return (iota((n, n), 0) == iota((n, n), 1)).astype(dtype)


def peers(n_dom, n_ch):
    return [(s, r, step) for s in range(n_ch) for r, step in ((0, 0), (1, -1), (2, 1)) if (s, r) != (0, 0)]


def greet(n_dom, n_ch):
    dom = lax.axis_index("dom")
    ch = lax.axis_index("ch")
    barrier = pltpu.get_barrier_semaphore()
    others = peers(n_dom, n_ch)
    for s, r, step in others:
        target = (lax.rem(dom + step + n_dom, n_dom), lax.rem(ch + s, n_ch))
        pl.semaphore_signal(barrier, inc=1, device_id=target, device_id_type=MESH)
    pl.semaphore_wait(barrier, len(others))
    return dom, ch


def share_kernel(n_dom, n_ch, node_ref, table_ref, own, send_sem, recv_sem, local_sem):
    count, group, atoms = node_ref.shape
    rows = node_ref[...].reshape(count * group, atoms)
    own[...] = nt(eye(atoms, BF), rows).astype(BF)
    dom, ch = greet(n_dom, n_ch)
    copies = []
    for s, r, step in peers(n_dom, n_ch):
        block = {0: 0, -1: 2, 1: 1}[step]
        copies.append(
            pltpu.make_async_remote_copy(
                src_ref=own,
                dst_ref=table_ref.at[ch, block],
                send_sem=send_sem.at[s, r],
                recv_sem=recv_sem.at[s, r],
                device_id=(lax.rem(dom + step + n_dom, n_dom), lax.rem(ch + s, n_ch)),
                device_id_type=MESH,
            )
        )
    for copy in copies:
        copy.start()
    mine = pltpu.make_async_copy(own, table_ref.at[ch, 0], local_sem)
    mine.start()
    mine.wait()
    for copy in copies:
        copy.wait()


def return_kernel(n_dom, n_ch, grads_ref, cot_ref, out_ref, landed, send_sem, recv_sem, local_sem):
    count, group, atoms = cot_ref.shape
    dom, ch = greet(n_dom, n_ch)
    copies = []
    for s, r, step in peers(n_dom, n_ch):
        other = lax.rem(ch + s, n_ch)
        copies.append(
            pltpu.make_async_remote_copy(
                src_ref=grads_ref.at[other, r],
                dst_ref=landed.at[ch, r],
                send_sem=send_sem.at[s, r],
                recv_sem=recv_sem.at[s, r],
                device_id=(lax.rem(dom + step + n_dom, n_dom), other),
                device_id_type=MESH,
            )
        )
    for copy in copies:
        copy.start()
    mine = pltpu.make_async_copy(grads_ref.at[ch, 0], landed.at[ch, 0], local_sem)
    mine.start()
    mine.wait()
    for copy in copies:
        copy.wait()
    total = n_ch * 3 * atoms
    terms = landed[...].reshape(total, count * group)
    pick = (lax.rem(iota((total, atoms), 0), atoms) == iota((total, atoms), 1)).astype(BF)
    summed = tn(terms, pick)
    out_ref[...] = cot_ref[...].astype(F32) + summed.reshape(count, group, atoms)


def roll_all(x, atoms, op):
    shift = atoms
    while shift < x.shape[1]:
        x = op(x, pltpu.roll(x, shift, 1))
        shift *= 2
    return x


def per_head(x, head):
    group, edges = x.shape
    total = jnp.sum(x.reshape(group // head, head, edges), axis=1, keepdims=True)
    return jnp.broadcast_to(total, (group // head, head, edges)).reshape(group, edges)


def work_kernel(
    head,
    table_ref,
    node_ref,
    cot_ref,
    source_ref,
    turn_ref,
    live_ref,
    ghost_ref,
    wig_ref,
    w0_ref,
    w1_ref,
    w2_ref,
    attn_ref,
    updated_ref,
    grads_ref,
    turned,
    feats,
    rot0,
    rot1,
    rot2,
    y_ref,
    cots,
    gy_ref,
    agg_ref,
):
    n_ch, _, atoms, width_all = table_ref.shape
    count, group, _ = node_ref.shape
    chans = n_ch * group
    slots = source_ref.shape[0]
    edges = slots * atoms
    rows = count * group
    rots = wig_ref.shape[1]

    spread_f = (lax.rem(iota((atoms, edges), 1), atoms) == iota((atoms, edges), 0)).astype(BF)
    mine = lax.div(iota((slots, edges), 1), atoms) == iota((slots, edges), 0)

    def lanes(ref):
        wide = nn(ref[...].astype(F32).astype(BF), spread_f)
        return jnp.sum(jnp.where(mine, wide, 0.0), axis=0, keepdims=True).astype(jnp.int32)

    source = lanes(source_ref)
    turn = lanes(turn_ref)
    counts = nn(jnp.broadcast_to(live_ref[...], (8, atoms)).astype(F32).astype(BF), spread_f)[:1]
    n_ghost = ghost_ref.shape[1]
    ghost_col = jnp.sum(
        eye(n_ghost, F32) * ghost_ref[...].astype(F32), axis=1, keepdims=True
    )
    picked = iota((n_ghost, edges), 0) == source - atoms
    ghost = jnp.sum(jnp.where(picked, ghost_col, 0.0), axis=0, keepdims=True).astype(jnp.int32)
    raw = jnp.where(
        source < atoms,
        source,
        jnp.where(source < atoms + n_ghost // 2, ghost + atoms, ghost + 2 * atoms),
    )
    pick = (iota((3 * atoms, edges), 0) == raw).astype(F32).astype(BF)
    pick_turn = (iota((rots, edges), 0) == turn).astype(F32).astype(BF)

    wig = wig_ref[...]
    high = wig.astype(BF)
    low = (wig - high.astype(F32)).astype(BF)
    turned[...] = nn(high, pick_turn) + nn(low, pick_turn)

    def coef(offset, width, row, col):
        at = offset + row * width + col
        return turned[at : at + 1, :]

    for p in range(n_ch):
        feats[p * rows : (p + 1) * rows, :] = tn(
            table_ref[p].reshape(3 * atoms, width_all), pick
        )
    cots[...] = nn(cot_ref[...].reshape(rows, atoms), spread_f)

    per = group // CHUNK

    def rot_slot(level, order, at, n):
        if order == 0:
            return 0, level * n + at, 0
        first = (level - abs(order)) * n + at
        return abs(order), first, 0 if order > 0 else edges

    rot_refs = (rot0, rot1, rot2)

    def rotate_in(i, carry):
        base = pl.multiple_of(lax.div(i, per) * rows + lax.rem(i, per) * CHUNK, CHUNK)
        at = pl.multiple_of(i * CHUNK, CHUNK)
        for level, width, offset, kept in BLOCKS:
            f = [
                feats[pl.ds(base + (level * level + q) * group, CHUNK), :] for q in range(width)
            ]
            for order in kept:
                acc = coef(offset, width, level + order, 0) * f[0]
                for q in range(1, width):
                    acc = acc + coef(offset, width, level + order, q) * f[q]
                which, row, lane = rot_slot(level, order, at, chans)
                rot_refs[which][pl.ds(row, CHUNK), lane : lane + edges] = acc.astype(BF)
        return carry

    lax.fori_loop(0, chans // CHUNK, rotate_in, 0)

    y_at = {}
    pos = 0
    for level in range(LMAX + 1):
        y_at[(level, 0)] = pos
        pos += group
    y_ref[0:pos, :] = nn(w0_ref[...], rot0[...])
    for order, w_ref, rot in ((1, w1_ref, rot1), (2, w2_ref, rot2)):
        n = (LMAX + 1 - order) * group
        both = nn(w_ref[...], rot[...])
        y_ref[pos : pos + n, :] = both[:n, :edges] - both[n:, edges:]
        y_ref[pos + n : pos + 2 * n, :] = both[:n, edges:] + both[n:, :edges]
        for level in range(order, LMAX + 1):
            y_at[(level, order)] = pos + (level - order) * group
            y_at[(level, -order)] = pos + n + (level - order) * group
        pos += 2 * n

    scalar = y_ref[0:group, :]
    sig = jax.nn.sigmoid(scalar)
    attn = jnp.sum(eye(group, F32) * attn_ref[...], axis=1, keepdims=True)
    score = per_head(scalar * sig * attn, head)
    live = lax.div(iota((group, edges), 1), atoms).astype(F32) < counts
    top = roll_all(jnp.where(live, score, -1e30), atoms, jnp.maximum)
    weight = jnp.exp(jnp.where(live, score - top, -1e30))
    weight = weight / roll_all(weight, atoms, jnp.add)

    gate = sig * weight
    proj = []
    for c in range(group // CHUNK):
        at = c * CHUNK
        gate_c = gate[at : at + CHUNK]
        total = jnp.zeros((CHUNK, edges), F32)
        for level, width, offset, kept in BLOCKS:
            ys = [y_ref[y_at[(level, o)] + at : y_at[(level, o)] + at + CHUNK, :] for o in kept]
            vs = [y * gate_c for y in ys]
            gs = [None] * len(kept)
            for q in range(width):
                k = (level * level + q) * group + at
                g = cots[k : k + CHUNK, :]
                acc = None
                for j, order in enumerate(kept):
                    d = coef(offset, width, level + order, q)
                    term = d * vs[j]
                    acc = term if acc is None else acc + term
                    back = d * g
                    gs[j] = back if gs[j] is None else gs[j] + back
                agg_ref[k : k + CHUNK, :] = acc.astype(BF)
            for j, order in enumerate(kept):
                total = total + gs[j] * ys[j]
                if (level, order) == (0, 0):
                    continue
                row = y_at[(level, order)] + at
                gy_ref[row : row + CHUNK, :] = (gs[j] * gate_c).astype(BF)
            if level == 0:
                first = gs[0] * gate_c
        proj.append((total, first))
    total = jnp.concatenate([t for t, _ in proj], axis=0)
    first = jnp.concatenate([f for _, f in proj], axis=0)
    dweight = per_head(sig * total, head)
    dscore = weight * (dweight - roll_all(weight * dweight, atoms, jnp.add))
    slope = sig * (1.0 - sig)
    first = first + weight * total * slope + dscore * attn * (sig + scalar * slope)
    gy_ref[0:group, :] = first.astype(BF)

    agg = nt(agg_ref[...], spread_f).reshape(count, group, atoms)
    updated_ref[...] = (node_ref[...].astype(F32) + agg).astype(BF)

    n0 = (LMAX + 1) * group
    rot0[...] = tn(w0_ref[...], gy_ref[0:n0, :]).astype(BF)
    pos = n0
    for order, w_ref, rot in ((1, w1_ref, rot1), (2, w2_ref, rot2)):
        n = (LMAX + 1 - order) * group
        plus = gy_ref[pos : pos + n, :]
        minus = gy_ref[pos + n : pos + 2 * n, :]
        both = jnp.concatenate(
            [jnp.concatenate([plus, minus], axis=1), jnp.concatenate([minus, -plus], axis=1)],
            axis=0,
        )
        rot[...] = tn(w_ref[...], both).astype(BF)
        pos += 2 * n

    def rotate_out(i, carry):
        base = pl.multiple_of(lax.div(i, per) * rows + lax.rem(i, per) * CHUNK, CHUNK)
        at = pl.multiple_of(i * CHUNK, CHUNK)
        for level, width, offset, kept in BLOCKS:
            ds = []
            for order in kept:
                which, row, lane = rot_slot(level, order, at, chans)
                ds.append(
                    rot_refs[which][pl.ds(row, CHUNK), lane : lane + edges].astype(F32)
                )
            for q in range(width):
                acc = None
                for j, order in enumerate(kept):
                    term = coef(offset, width, level + order, q) * ds[j]
                    acc = term if acc is None else acc + term
                feats[pl.ds(base + (level * level + q) * group, CHUNK), :] = acc
        return carry

    lax.fori_loop(0, chans // CHUNK, rotate_out, 0)
    for p in range(n_ch):
        part = feats[p * rows : (p + 1) * rows, :].astype(BF)
        grads_ref[p] = nt(pick, part).astype(BF).reshape(3, atoms, width_all)


def on_device(
    n_dom,
    n_ch,
    node_irreps,
    out_grad,
    edge_source,
    edge_rotation,
    edge_count,
    ghost_slot,
    wigner,
    so2_m0,
    so2_m1,
    so2_m2,
    attn_vector,
):
    count, group, atoms = node_irreps.shape
    chans = n_ch * group
    slots = edge_source.shape[0]
    edges = slots * atoms
    rows = count * group
    vmem = pl.BlockSpec(memory_space=VMEM)
    blocks = jax.ShapeDtypeStruct((n_ch, 3, atoms, rows), BF)
    sems = [
        pltpu.SemaphoreType.DMA((n_ch, 3)),
        pltpu.SemaphoreType.DMA((n_ch, 3)),
        pltpu.SemaphoreType.DMA,
    ]
    table = pl.pallas_call(
        functools.partial(share_kernel, n_dom, n_ch),
        out_shape=blocks,
        in_specs=[vmem],
        out_specs=vmem,
        scratch_shapes=[VMEM((atoms, rows), BF)] + sems,
        compiler_params=pltpu.CompilerParams(collective_id=0, has_side_effects=True),
        name="share",
    )(node_irreps)
    n_pairs = sum(len(b[3]) for b in BLOCKS)
    updated, grads = pl.pallas_call(
        functools.partial(work_kernel, chans // HEADS),
        out_shape=(jax.ShapeDtypeStruct(node_irreps.shape, BF), blocks),
        in_specs=[vmem] * 12,
        out_specs=(vmem, vmem),
        scratch_shapes=[
            VMEM((wigner.shape[0], edges), F32),
            VMEM((n_ch * rows, edges), F32),
            VMEM(((LMAX + 1) * chans, edges), BF),
            VMEM((LMAX * chans, 2 * edges), BF),
            VMEM(((LMAX - 1) * chans, 2 * edges), BF),
            VMEM((n_pairs * group, edges), F32),
            VMEM((rows, edges), F32),
            VMEM((n_pairs * group, edges), BF),
            VMEM((rows, edges), BF),
        ],
        compiler_params=pltpu.CompilerParams(vmem_limit_bytes=56 * 1024 * 1024),
        name="work",
    )(
        table,
        node_irreps,
        out_grad,
        edge_source,
        edge_rotation,
        edge_count.reshape(1, atoms),
        ghost_slot.reshape(1, -1),
        wigner,
        so2_m0.reshape((LMAX + 1) * group, (LMAX + 1) * chans),
        so2_m1.reshape(2 * LMAX * group, LMAX * chans),
        so2_m2.reshape(2 * (LMAX - 1) * group, (LMAX - 1) * chans),
        attn_vector.reshape(1, group),
    )
    irreps_grad = pl.pallas_call(
        functools.partial(return_kernel, n_dom, n_ch),
        out_shape=jax.ShapeDtypeStruct(node_irreps.shape, F32),
        in_specs=[vmem, vmem],
        out_specs=vmem,
        scratch_shapes=[VMEM(blocks.shape, BF)] + sems,
        compiler_params=pltpu.CompilerParams(collective_id=1, has_side_effects=True),
        name="give_back",
    )(grads, out_grad)
    return (updated, irreps_grad)


def solution(mesh):
    placed = (
        P(None, "ch", "dom"),
        P(None, "ch", "dom"),
        P(None, "dom"),
        P(None, "dom"),
        P("dom"),
        P("dom"),
        P(None, "dom"),
        P(None, "ch", None, None),
        P(None, None, "ch", None, None),
        P(None, None, "ch", None, None),
        P("ch"),
    )
    return jax.shard_map(
        functools.partial(on_device, mesh.shape["dom"], mesh.shape["ch"]),
        mesh=mesh,
        in_specs=placed,
        out_specs=(P(None, "ch", "dom"), P(None, "ch", "dom")),
        check_vma=False,
    )
```

```python
import functools

import jax
import jax.numpy as jnp
from jax import lax
from jax.experimental import pallas as pl
from jax.experimental.pallas import tpu as pltpu
from jax.sharding import PartitionSpec as P

HEADS = 8
LMAX = 6
MMAX = 2
CHUNK = 16
MESH = pl.DeviceIdType.MESH
VMEM = pltpu.VMEM
BF = jnp.bfloat16
F32 = jnp.float32


def degree_blocks():
    out = []
    offset = 0
    for level in range(LMAX + 1):
        width = 2 * level + 1
        reach = min(level, MMAX)
        out.append((level, width, offset, list(range(-reach, reach + 1))))
        offset += width * width
    return out


BLOCKS = degree_blocks()


def dot(a, b, dims):
    return lax.dot_general(a, b, (dims, ((), ())), preferred_element_type=F32)


def nn(a, b):
    return dot(a, b, ((1,), (0,)))


def nt(a, b):
    return dot(a, b, ((1,), (1,)))


def tn(a, b):
    return dot(a, b, ((0,), (0,)))


def iota(shape, dim):
    return lax.broadcasted_iota(jnp.int32, shape, dim)


def eye(n, dtype):
    return (iota((n, n), 0) == iota((n, n), 1)).astype(dtype)


def roll_all(x, atoms, op):
    shift = atoms
    while shift < x.shape[1]:
        x = op(x, pltpu.roll(x, shift, 1))
        shift *= 2
    return x


def per_head(x, head):
    group, edges = x.shape
    total = jnp.sum(x.reshape(group // head, head, edges), axis=1, keepdims=True)
    return jnp.broadcast_to(total, (group // head, head, edges)).reshape(group, edges)


def kernel(
    n_dom,
    n_ch,
    head,
    node_ref,
    source_ref,
    turn_ref,
    live_ref,
    ghost_ref,
    attn_ref,
    cot_hbm,
    wig_hbm,
    w0_hbm,
    w1_hbm,
    w2_hbm,
    updated_ref,
    out_ref,
    cot_ref,
    wig_ref,
    w0,
    w1,
    w2,
    table_ref,
    grads_ref,
    landed,
    sums,
    partial,
    flat,
    flat_cot,
    turned,
    feats,
    rot0,
    rot1,
    rot2,
    y_ref,
    cots,
    gy_ref,
    agg_ref,
    dfeats,
    load_sem,
    table_sem,
    ring_sem,
    back_sem,
    sum_sem,
):
    count, atoms, group = node_ref.shape
    chans = n_ch * group
    slots = source_ref.shape[0]
    edges = slots * atoms
    rows = count * group
    rots = wig_ref.shape[1]
    dom = lax.axis_index("dom")
    ch = lax.axis_index("ch")
    lower = lax.rem(dom + n_dom - 1, n_dom)
    upper = lax.rem(dom + 1, n_dom)

    load_cot = pltpu.make_async_copy(cot_hbm, cot_ref, load_sem.at[0])
    load_wig = pltpu.make_async_copy(wig_hbm, wig_ref, load_sem.at[1])
    load_wig.start()
    load_cot.start()
    load_w = []
    for hbm, ref in ((w0_hbm, w0), (w1_hbm, w1), (w2_hbm, w2)):
        for level in range(hbm.shape[-3]):
            lanes_of = slice(level * chans, (level + 1) * chans)
            if hbm.ndim == 4:
                one, place = hbm.at[:, level], ref.at[:, :, lanes_of]
            else:
                one, place = hbm.at[:, :, level], ref.at[:, :, :, lanes_of]
            load_w.append(pltpu.make_async_copy(one, place, load_sem.at[2 + len(load_w)]))
            load_w[-1].start()

    for k in range(count):
        table_ref[ch, 0, :, k * group : (k + 1) * group] = node_ref[k]

    def remote(source, target, sems, place, device):
        return pltpu.make_async_remote_copy(
            src_ref=source,
            dst_ref=target,
            send_sem=sems.at[(0,) + place],
            recv_sem=sems.at[(1,) + place],
            device_id=device,
            device_id_type=MESH,
        )

    barrier = pltpu.get_barrier_semaphore()
    partners = [(dom, lax.rem(ch + s, n_ch)) for s in range(1, n_ch)]
    for target in [(lower, ch), (upper, ch)] + partners:
        pl.semaphore_signal(barrier, inc=1, device_id=target, device_id_type=MESH)
    pl.semaphore_wait(barrier, n_ch + 1)

    own = table_ref.at[ch, 0]
    across = [remote(own, own, table_sem, (s,), partners[s - 1]) for s in range(1, n_ch)]
    for copy in across:
        copy.start()

    def pass_on(q, s):
        both = [
            remote(table_ref.at[q, 0], table_ref.at[q, 2], ring_sem, (s, 0), (lower, ch)),
            remote(table_ref.at[q, 0], table_ref.at[q, 1], ring_sem, (s, 1), (upper, ch)),
        ]
        for copy in both:
            copy.start()
        return both

    along = pass_on(ch, 0)

    spread_f = (lax.rem(iota((atoms, edges), 1), atoms) == iota((atoms, edges), 0)).astype(BF)
    mine = lax.div(iota((slots, edges), 1), atoms) == iota((slots, edges), 0)

    def lanes(ref):
        wide = nn(ref[...].astype(F32).astype(BF), spread_f)
        return jnp.sum(jnp.where(mine, wide, 0.0), axis=0, keepdims=True).astype(jnp.int32)

    source = lanes(source_ref)
    turn = lanes(turn_ref)
    counts = nn(jnp.broadcast_to(live_ref[...], (8, atoms)).astype(F32).astype(BF), spread_f)[:1]
    n_ghost = ghost_ref.shape[1]
    ghost_col = jnp.sum(
        eye(n_ghost, F32) * ghost_ref[...].astype(F32), axis=1, keepdims=True
    )
    picked = iota((n_ghost, edges), 0) == source - atoms
    ghost = jnp.sum(jnp.where(picked, ghost_col, 0.0), axis=0, keepdims=True).astype(jnp.int32)
    raw = jnp.where(
        source < atoms,
        source,
        jnp.where(source < atoms + n_ghost // 2, ghost + atoms, ghost + 2 * atoms),
    )
    pick = (iota((3 * atoms, edges), 0) == raw).astype(F32).astype(BF)
    pick_turn = (iota((rots, edges), 0) == turn).astype(F32).astype(BF)

    load_wig.wait()
    wig = wig_ref[...]
    high = wig.astype(BF)
    low = (wig - high.astype(F32)).astype(BF)
    turned[...] = nn(high, pick_turn) + nn(low, pick_turn)

    def coef(offset, width, row, col):
        at = offset + row * width + col
        return turned[at : at + 1, :]

    for s in range(1, n_ch):
        across[s - 1].wait_recv()
        along += pass_on(lax.rem(ch + n_ch - s, n_ch), s)

    load_cot.wait()
    for k in range(count):
        flat_cot[:, k * group : (k + 1) * group] = cot_ref[k]
    cots[...] = tn(flat_cot[...], spread_f)

    for copy in along:
        copy.wait_recv()
    for p in range(n_ch):
        feats[p * rows : (p + 1) * rows, :] = tn(
            table_ref[p].reshape(3 * atoms, rows), pick
        )

    per = group // CHUNK

    def rot_slot(level, order, at, n):
        if order == 0:
            return 0, level * n + at, 0
        first = (level - abs(order)) * n + at
        return abs(order), first, 0 if order > 0 else edges

    rot_refs = (rot0, rot1, rot2)

    def rotate_in(i, carry):
        base = pl.multiple_of(lax.div(i, per) * rows + lax.rem(i, per) * CHUNK, CHUNK)
        at = pl.multiple_of(i * CHUNK, CHUNK)
        for level, width, offset, kept in BLOCKS:
            f = [
                feats[pl.ds(base + (level * level + q) * group, CHUNK), :] for q in range(width)
            ]
            for order in kept:
                acc = coef(offset, width, level + order, 0) * f[0]
                for q in range(1, width):
                    acc = acc + coef(offset, width, level + order, q) * f[q]
                which, row, lane = rot_slot(level, order, at, chans)
                rot_refs[which][pl.ds(row, CHUNK), lane : lane + edges] = acc.astype(BF)
        return carry

    lax.fori_loop(0, chans // CHUNK, rotate_in, 0)

    for copy in load_w:
        copy.wait()
    w0_ref = w0[...].reshape((LMAX + 1) * group, (LMAX + 1) * chans)
    w1_ref = w1[...].reshape(2 * LMAX * group, LMAX * chans)
    w2_ref = w2[...].reshape(2 * (LMAX - 1) * group, (LMAX - 1) * chans)
    y_at = {}
    pos = 0
    for level in range(LMAX + 1):
        y_at[(level, 0)] = pos
        pos += group
    y_ref[0:pos, :] = nn(w0_ref, rot0[...])
    for order, w_ref, rot in ((1, w1_ref, rot1), (2, w2_ref, rot2)):
        n = (LMAX + 1 - order) * group
        both = nn(w_ref, rot[...])
        y_ref[pos : pos + n, :] = both[:n, :edges] - both[n:, edges:]
        y_ref[pos + n : pos + 2 * n, :] = both[:n, edges:] + both[n:, :edges]
        for level in range(order, LMAX + 1):
            y_at[(level, order)] = pos + (level - order) * group
            y_at[(level, -order)] = pos + n + (level - order) * group
        pos += 2 * n

    scalar = y_ref[0:group, :]
    sig = jax.nn.sigmoid(scalar)
    attn = jnp.sum(eye(group, F32) * attn_ref[...], axis=1, keepdims=True)
    score = per_head(scalar * sig * attn, head)
    live = lax.div(iota((group, edges), 1), atoms).astype(F32) < counts
    top = roll_all(jnp.where(live, score, -1e30), atoms, jnp.maximum)
    weight = jnp.exp(jnp.where(live, score - top, -1e30))
    weight = weight / roll_all(weight, atoms, jnp.add)

    gate = sig * weight
    proj = []
    for c in range(group // CHUNK):
        at = c * CHUNK
        gate_c = gate[at : at + CHUNK]
        total = jnp.zeros((CHUNK, edges), F32)
        for level, width, offset, kept in BLOCKS:
            ys = [y_ref[y_at[(level, o)] + at : y_at[(level, o)] + at + CHUNK, :] for o in kept]
            vs = [y * gate_c for y in ys]
            gs = [None] * len(kept)
            for q in range(width):
                k = (level * level + q) * group + at
                g = cots[k : k + CHUNK, :]
                acc = None
                for j, order in enumerate(kept):
                    d = coef(offset, width, level + order, q)
                    term = d * vs[j]
                    acc = term if acc is None else acc + term
                    back = d * g
                    gs[j] = back if gs[j] is None else gs[j] + back
                agg_ref[k : k + CHUNK, :] = acc.astype(BF)
            for j, order in enumerate(kept):
                total = total + gs[j] * ys[j]
                if (level, order) == (0, 0):
                    continue
                row = y_at[(level, order)] + at
                gy_ref[row : row + CHUNK, :] = (gs[j] * gate_c).astype(BF)
            if level == 0:
                first = gs[0] * gate_c
        proj.append((total, first))
    total = jnp.concatenate([t for t, _ in proj], axis=0)
    first = jnp.concatenate([f for _, f in proj], axis=0)
    dweight = per_head(sig * total, head)
    dscore = weight * (dweight - roll_all(weight * dweight, atoms, jnp.add))
    slope = sig * (1.0 - sig)
    first = first + weight * total * slope + dscore * attn * (sig + scalar * slope)
    gy_ref[0:group, :] = first.astype(BF)

    n0 = (LMAX + 1) * group
    rot0[...] = tn(w0_ref, gy_ref[0:n0, :]).astype(BF)
    pos = n0
    for order, w_ref, rot in ((1, w1_ref, rot1), (2, w2_ref, rot2)):
        n = (LMAX + 1 - order) * group
        plus = gy_ref[pos : pos + n, :]
        minus = gy_ref[pos + n : pos + 2 * n, :]
        both = jnp.concatenate(
            [jnp.concatenate([plus, minus], axis=1), jnp.concatenate([minus, -plus], axis=1)],
            axis=0,
        )
        rot[...] = tn(w_ref, both).astype(BF)
        pos += 2 * n

    def rotate_out(p, i, carry):
        base = pl.multiple_of(i * CHUNK, CHUNK)
        at = pl.multiple_of(p * group + i * CHUNK, CHUNK)
        for level, width, offset, kept in BLOCKS:
            ds = []
            for order in kept:
                which, row, lane = rot_slot(level, order, at, chans)
                ds.append(
                    rot_refs[which][pl.ds(row, CHUNK), lane : lane + edges].astype(F32)
                )
            for q in range(width):
                acc = None
                for j, order in enumerate(kept):
                    term = coef(offset, width, level + order, q) * ds[j]
                    acc = term if acc is None else acc + term
                dfeats[pl.ds(base + (level * level + q) * group, CHUNK), :] = acc.astype(BF)
        return carry

    homeward = []
    for s in list(range(1, n_ch)) + [0]:
        p = lax.rem(ch + s, n_ch)
        lax.fori_loop(0, per, functools.partial(rotate_out, p), 0)
        grads_ref[p] = nt(pick, dfeats[...]).astype(BF).reshape(3, atoms, rows)
        both = [
            remote(grads_ref.at[p, 1], landed.at[p, 1], back_sem, (s, 0), (lower, ch)),
            remote(grads_ref.at[p, 2], landed.at[p, 0], back_sem, (s, 1), (upper, ch)),
        ]
        for copy in both:
            copy.start()
        homeward.append((s, p, both))

    flat[...] = nt(spread_f, agg_ref[...])
    for k in range(count):
        mine_k = node_ref[k].astype(F32) + flat[:, k * group : (k + 1) * group]
        updated_ref[k] = mine_k.astype(BF)

    last = []
    for s, p, both in homeward:
        for copy in both:
            copy.wait_recv()
        total = (
            grads_ref[p, 0].astype(F32)
            + landed[p, 0].astype(F32)
            + landed[p, 1].astype(F32)
        )
        if s > 0:
            partial[s - 1] = total.astype(BF)
            copy = remote(partial.at[s - 1], sums.at[s - 1], sum_sem, (s,), (dom, p))
            copy.start()
            last.append(copy)
    for copy in last:
        copy.wait_recv()
    for s in range(1, n_ch):
        total = total + sums[s - 1].astype(F32)
    flat[...] = total
    for k in range(count):
        out_ref[k] = cot_ref[k].astype(F32) + flat[:, k * group : (k + 1) * group]
    for copy in across + along + [c for h in homeward for c in h[2]] + last:
        copy.wait_send()


def on_device(
    n_dom,
    n_ch,
    node_irreps,
    out_grad,
    edge_source,
    edge_rotation,
    edge_count,
    ghost_slot,
    wigner,
    so2_m0,
    so2_m1,
    so2_m2,
    attn_vector,
):
    count, group, atoms = node_irreps.shape
    chans = n_ch * group
    slots = edge_source.shape[0]
    edges = slots * atoms
    rows = count * group
    vmem = pl.BlockSpec(memory_space=VMEM)
    anywhere = pl.BlockSpec(memory_space=pl.ANY)
    n_pairs = sum(len(b[3]) for b in BLOCKS)
    dma = pltpu.SemaphoreType.DMA
    flipped = (count, atoms, group)
    updated, irreps_grad = pl.pallas_call(
        functools.partial(kernel, n_dom, n_ch, chans // HEADS),
        out_shape=(jax.ShapeDtypeStruct(flipped, BF), jax.ShapeDtypeStruct(flipped, F32)),
        in_specs=[vmem] * 6 + [anywhere] * 5,
        out_specs=(vmem, vmem),
        scratch_shapes=[
            VMEM(flipped, BF),
            VMEM(wigner.shape, F32),
            VMEM((LMAX + 1, group, (LMAX + 1) * chans), BF),
            VMEM((2, LMAX, group, LMAX * chans), BF),
            VMEM((2, LMAX - 1, group, (LMAX - 1) * chans), BF),
            VMEM((n_ch, 3, atoms, rows), BF),
            VMEM((n_ch, 3, atoms, rows), BF),
            VMEM((n_ch, 2, atoms, rows), BF),
            VMEM((max(n_ch - 1, 1), atoms, rows), BF),
            VMEM((max(n_ch - 1, 1), atoms, rows), BF),
            VMEM((atoms, rows), F32),
            VMEM((atoms, rows), BF),
            VMEM((wigner.shape[0], edges), F32),
            VMEM((n_ch * rows, edges), F32),
            VMEM(((LMAX + 1) * chans, edges), BF),
            VMEM((LMAX * chans, 2 * edges), BF),
            VMEM(((LMAX - 1) * chans, 2 * edges), BF),
            VMEM((n_pairs * group, edges), F32),
            VMEM((rows, edges), F32),
            VMEM((n_pairs * group, edges), BF),
            VMEM((rows, edges), BF),
            VMEM((rows, edges), BF),
            dma((2 + 3 * LMAX,)),
            dma((2, n_ch)),
            dma((2, n_ch, 2)),
            dma((2, n_ch, 2)),
            dma((2, n_ch)),
        ],
        compiler_params=pltpu.CompilerParams(
            collective_id=0, has_side_effects=True, vmem_limit_bytes=56 * 1024 * 1024
        ),
        name="layer",
    )(
        jnp.transpose(node_irreps, (0, 2, 1)),
        edge_source,
        edge_rotation,
        edge_count.reshape(1, atoms),
        ghost_slot.reshape(1, -1),
        attn_vector.reshape(1, group),
        jnp.transpose(out_grad, (0, 2, 1)),
        wigner,
        jnp.transpose(so2_m0, (0, 2, 1, 3)),
        jnp.transpose(so2_m1, (0, 1, 3, 2, 4)),
        jnp.transpose(so2_m2, (0, 1, 3, 2, 4)),
    )
    return (jnp.transpose(updated, (0, 2, 1)), jnp.transpose(irreps_grad, (0, 2, 1)))


def solution(mesh):
    placed = (
        P(None, "ch", "dom"),
        P(None, "ch", "dom"),
        P(None, "dom"),
        P(None, "dom"),
        P("dom"),
        P("dom"),
        P(None, "dom"),
        P(None, "ch", None, None),
        P(None, None, "ch", None, None),
        P(None, None, "ch", None, None),
        P("ch"),
    )
    return jax.shard_map(
        functools.partial(on_device, mesh.shape["dom"], mesh.shape["ch"]),
        mesh=mesh,
        in_specs=placed,
        out_specs=(P(None, "ch", "dom"), P(None, "ch", "dom")),
        check_vma=False,
    )
```
